768 devices in a mesh: lon: 32 (over z_hi, y), lat: 24 (over x, z_lo, core).
Axes of the slice: x: 4, y: 8, z: 12 (z_hi: 4, z_lo: 3; z = z_hi * 3 + z_lo), core: 2. Of those that a mesh axis runs over, the one named last changes fastest.
Arguments:
- fields: bfloat16 [384, 1024, 128], P('lat', 'lon'), may hold values from -6 to 6
- cotangent: bfloat16 [384, 1024, 128], P('lat', 'lon'), may hold values from -6 to 6
- weight_first: bfloat16 [3, 3, 128, 128], replicated, may hold values from -0.1875 to 0.1875
- weight_second: bfloat16 [3, 3, 128, 128], replicated, may hold values from -0.1875 to 0.1875
Outputs:
- output: bfloat16 [384, 1024, 128], P('lat', 'lon')
- back_fields: bfloat16 [384, 1024, 128], P('lat', 'lon')
- grad_first: float32 [3, 3, 128, 128], replicated
- grad_second: float32 [3, 3, 128, 128], replicated
The draws below stay inside these ranges and needn't reach their ends.
All inputs are finite; a program needn't handle non-finite values.
Results may differ from the reference program's by a relative error of at most 0.0034.
Values may be sent and summed in bfloat16 or wider, within the bound.
No kernel may reach another device: no remote copies, remote signals or barrier semaphores. Data moves between devices by JAX's collectives and lax.ppermute only.
A program may use at most 32 MiB of HBM per device.

```python
import math
import jax
import jax.numpy as jnp

C = 128
NLAT = 384
NLON = 1024


def steps_of(key, shape, shards, low, top_value):
    def one(dim, blocks):
        steps = jax.random.uniform(jax.random.fold_in(jax.random.fold_in(key, 6), dim), (blocks,), jnp.float32, low / len(shards), top_value / len(shards))
        return jnp.repeat(jnp.exp(steps), shape[dim] // blocks).reshape((-1,) + (1,) * (len(shape) - dim - 1))

    loudness = one(*shards[0])
    for cut in shards[1:]:
        loudness = loudness * one(*cut)
    return loudness


def gaussian(own_key, extent, width, reach, shards=(), dtype=jnp.bfloat16):
    entries = width * jax.random.normal(own_key, extent, jnp.float32)
    if shards:
        entries = entries * steps_of(own_key, extent, shards, -0.22, 0.18)
    return jnp.clip(entries, -reach, reach).astype(dtype)


def setup_inputs(seed: int = 0) -> dict:
    key_list = jax.random.split(jax.random.key(seed), 5)
    fields = gaussian(key_list[0], (NLAT, NLON, C), 1.0, 6.0, ((0, 24), (1, 32)))
    cotangent = gaussian(key_list[1], (NLAT, NLON, C), 1.0, 6.0, ((0, 24), (1, 32)))
    weight_first = gaussian(key_list[2], (3, 3, C, C), (9 * C) ** -0.5, 0.1875)
    weight_second = gaussian(key_list[3], (3, 3, C, C), (9 * C) ** -0.5, 0.1875)
    return {"fields": fields, "cotangent": cotangent, "weight_first": weight_first, "weight_second": weight_second}


def extend(field):
    half_way = field.shape[1] // 2
    top_row = jnp.roll(field[0:1], -half_way, axis=1)
    bottom_row = jnp.roll(field[-1:], -half_way, axis=1)
    with_rows = jnp.concatenate([top_row, field, bottom_row], axis=0)
    return jnp.concatenate([with_rows[:, -1:], with_rows, with_rows[:, :1]], axis=1)

def fold_back(padded):
    half_way = (padded.shape[1] - 2) // 2
    with_rows = padded[:, 1:-1]
    with_rows = with_rows.at[:, -1].add(padded[:, 0])
    with_rows = with_rows.at[:, 0].add(padded[:, -1])
    interior = with_rows[1:-1]
    interior = interior.at[0].add(jnp.roll(with_rows[0], half_way, axis=0))
    interior = interior.at[-1].add(jnp.roll(with_rows[-1], half_way, axis=0))
    return interior

def convolve(field, weight):
    lat_count, lon_count, channels = field.shape
    padded = extend(field)
    summed = jnp.zeros((lat_count * lon_count, channels), jnp.float32)
    for tap_row in range(3):
        for tap_col in range(3):
            piece = padded[tap_row:tap_row + lat_count, tap_col:tap_col + lon_count].reshape(-1, channels)
            summed = summed + jnp.dot(piece, weight[tap_row, tap_col], preferred_element_type=jnp.float32)
    return summed.reshape(lat_count, lon_count, channels)

def adjoint(upstream, weight):
    lat_count, lon_count, channels = upstream.shape
    flat_up = upstream.reshape(-1, channels)
    padded = jnp.zeros((lat_count + 2, lon_count + 2, channels), jnp.float32)
    for tap_row in range(3):
        for tap_col in range(3):
            term = jnp.dot(flat_up, weight[tap_row, tap_col].T, preferred_element_type=jnp.float32)
            padded = padded.at[tap_row:tap_row + lat_count, tap_col:tap_col + lon_count].add(term.reshape(lat_count, lon_count, channels))
    return fold_back(padded)

def weight_grad(field, upstream):
    lat_count, lon_count, channels = field.shape
    padded = extend(field)
    flat_up = upstream.reshape(-1, channels)
    rows_out = []
    for tap_row in range(3):
        cols_out = []
        for tap_col in range(3):
            piece = padded[tap_row:tap_row + lat_count, tap_col:tap_col + lon_count].reshape(-1, channels)
            cols_out.append(jnp.dot(piece.T, flat_up, preferred_element_type=jnp.float32))
        rows_out.append(jnp.stack(cols_out))
    return jnp.stack(rows_out)

def reference(fields, cotangent, weight_first, weight_second):
    first_sum = convolve(fields, weight_first)
    hidden = jax.nn.silu(first_sum).astype(jnp.bfloat16)
    second_sum = convolve(hidden, weight_second)
    output = (fields.astype(jnp.float32) + second_sum).astype(jnp.bfloat16)
    grad_scale = 1.0 / math.sqrt(NLAT * NLON)
    grad_second = weight_grad(hidden, cotangent) * grad_scale
    back_hidden = adjoint(cotangent, weight_second)
    sigmoid_first = jax.nn.sigmoid(first_sum)
    back_first = (back_hidden * sigmoid_first * (1.0 + first_sum * (1.0 - sigmoid_first))).astype(jnp.bfloat16)
    grad_first = weight_grad(fields, back_first) * grad_scale
    back_fields = (cotangent.astype(jnp.float32) + adjoint(back_first, weight_first)).astype(jnp.bfloat16)
    return (output, back_fields, grad_first, grad_second)
```

```python
import math

import jax
import jax.numpy as jnp
from jax import lax
from jax.sharding import Mesh, PartitionSpec as P

LON = ("zh", "y")
LAT = ("x", "zl", "core")
SIZES = {"zh": 4, "y": 8, "x": 4, "zl": 3, "core": 2}
SCATTER = (("core", jnp.float32), (("y", "x"), jnp.bfloat16))
EXCHANGE = ("zh", "zl")


def swap(x, partner):
    lats, lons = lax.axis_size(LAT), lax.axis_size(LON)
    pairs = []
    for j in range(lons):
        for i in range(lats):
            to_lat, to_lon = partner(i, j)
            pairs.append((j * lats + i, (to_lon % lons) * lats + to_lat))
    return lax.ppermute(x, LON + LAT, pairs)


def halo_of_two(stack, north_pole, south_pole):
    lats, lons = lax.axis_size(LAT), lax.axis_size(LON)
    rows, cols = stack.shape[1:3]
    odd_row = lax.axis_index(LAT) % 2 == 1
    odd_col = lax.axis_index(LON) % 2 == 1

    def across_chips(i, j):
        to = i + 1 if i % 2 else i - 1
        return (to, j) if 0 <= to < lats else (i, j + lons // 2)

    top, bottom = stack[:, :2], stack[:, rows - 2 :]
    outer = swap(jnp.where(odd_row, bottom, top), across_chips)
    inner = swap(jnp.where(odd_row, top, bottom), lambda i, j: (i - 1 if i % 2 else i + 1, j))
    outer = jnp.where(north_pole | south_pole, outer[:, ::-1], outer)
    above = jnp.where(odd_row, inner, outer)
    below = jnp.where(odd_row, outer, inner)
    tall = jnp.concatenate([above, stack, below], axis=1)
    first, last = tall[:, :, :2], tall[:, :, cols - 2 :]
    far = swap(jnp.where(odd_col, last, first), lambda i, j: (i, j + 1 if j % 2 else j - 1))
    near = swap(jnp.where(odd_col, first, last), lambda i, j: (i, j - 1 if j % 2 else j + 1))
    left = jnp.where(odd_col, near, far)
    right = jnp.where(odd_col, far, near)
    return jnp.concatenate([left, tall, right], axis=2)


def tap_patches(padded):
    row_count, col_count = padded.shape[0] - 2, padded.shape[1] - 2
    return jnp.concatenate(
        [
            padded[tap_row : tap_row + row_count, tap_col : tap_col + col_count]
            for tap_row in range(3)
            for tap_col in range(3)
        ],
        axis=-1,
    )


def apply_kernel(patches, weight):
    return jnp.einsum(
        "rlk,kd->rld", patches, weight.reshape(-1, weight.shape[-1]), preferred_element_type=jnp.float32
    )


def outer_sums(patches, upstream):
    return jnp.einsum("rlk,rld->kd", patches, upstream, preferred_element_type=jnp.float32)


def turned(weight):
    return jnp.transpose(weight[::-1, ::-1], (0, 1, 3, 2))


def adjoint_rows(patches, weight, edge_rows, north_pole, south_pole):
    flipped = turned(weight)
    top = jnp.concatenate([jnp.where(north_pole, flipped[2:3], flipped[0:1]), flipped[1:]])
    bottom = jnp.concatenate([flipped[:2], jnp.where(south_pole, flipped[0:1], flipped[2:3])])
    return jnp.concatenate(
        [
            apply_kernel(patches[:edge_rows], top),
            apply_kernel(patches[edge_rows:-edge_rows], flipped),
            apply_kernel(patches[-edge_rows:], bottom),
        ]
    )


def all_sum(x):
    def exchange(v, axes):
        return lax.all_to_all(v, axes, 0, 0, tiled=True)

    def to_all(v, axes):
        return exchange(jnp.broadcast_to(v[None], (lax.axis_size(axes),) + v.shape), axes)

    piece = x
    for axes, dtype in SCATTER:
        pieces = piece.astype(dtype).reshape(lax.axis_size(axes), -1, x.shape[-1])
        piece = jnp.sum(exchange(pieces, axes).astype(jnp.float32), axis=0)
    piece = jnp.sum(to_all(piece, EXCHANGE), axis=0).astype(jnp.bfloat16)
    for axes, dtype in SCATTER[::-1]:
        piece = to_all(piece, axes).reshape(-1, x.shape[-1])
    return piece.astype(jnp.float32)


def per_device(fields, cotangent, weight_first, weight_second):
    row_count, col_count, channels = fields.shape
    lat_place = lax.axis_index(LAT)
    north_pole = lat_place == 0
    south_pole = lat_place == lax.axis_size(LAT) - 1
    extended = halo_of_two(jnp.stack([fields, cotangent]), north_pole, south_pole)

    patches_fields = tap_patches(extended[0])
    reversed_first = weight_first[::-1]
    first_sum = jnp.concatenate(
        [
            apply_kernel(patches_fields[:1], jnp.where(north_pole, reversed_first, weight_first)),
            apply_kernel(patches_fields[1:-1], weight_first),
            apply_kernel(patches_fields[-1:], jnp.where(south_pole, reversed_first, weight_first)),
        ]
    )
    hidden = jax.nn.silu(first_sum).astype(jnp.bfloat16)
    back_hidden = adjoint_rows(tap_patches(extended[1]), weight_second, 2, north_pole, south_pole)
    sigmoid_first = jax.nn.sigmoid(first_sum)
    back_first = (back_hidden * sigmoid_first * (1.0 + first_sum * (1.0 - sigmoid_first))).astype(
        jnp.bfloat16
    )
    patches_hidden = tap_patches(hidden)
    cells_total = row_count * lax.axis_size(LAT) * col_count * lax.axis_size(LON)
    grad_scale = 1.0 / math.sqrt(cells_total)
    grad_first = outer_sums(patches_fields[1:-1, 1:-1], back_first[1:-1, 1:-1])
    grad_second = outer_sums(patches_hidden, cotangent)
    grads = all_sum(jnp.concatenate([grad_first, grad_second])) * grad_scale
    grad_first, grad_second = (
        part.reshape(weight_first.shape) for part in jnp.split(grads, 2)
    )
    second_sum = apply_kernel(patches_hidden, weight_second)
    output = (fields.astype(jnp.float32) + second_sum).astype(jnp.bfloat16)
    back_fields = (
        cotangent.astype(jnp.float32)
        + adjoint_rows(tap_patches(back_first), weight_first, 1, north_pole, south_pole)
    ).astype(jnp.bfloat16)
    return (output, back_fields, grad_first, grad_second)


def solution(mesh):
    fine = Mesh(mesh.devices.reshape(tuple(SIZES.values())), tuple(SIZES))
    cells = P(LAT, LON, None)
    return jax.shard_map(
        per_device,
        mesh=fine,
        in_specs=(cells, cells, P(), P()),
        out_specs=(cells, cells, P(), P()),
        check_vma=False,
    )
```

```python
import math

import jax
import jax.numpy as jnp
from jax import lax
from jax.sharding import Mesh, PartitionSpec as P


LON = ("zh", "y")
LAT = ("x", "zl", "core")
SIZES = {"zh": 4, "y": 8, "x": 4, "zl": 3, "core": 2}
SCATTER = ("y", "x")
EXCHANGE = ("zh", "zl")


def swap(x, partner):
    lats, lons = lax.axis_size(LAT), lax.axis_size(LON)
    pairs = []
    for j in range(lons):
        for i in range(lats):
            to_lat, to_lon = partner(i, j)
            pairs.append((j * lats + i, (to_lon % lons) * lats + to_lat))
    return lax.ppermute(x, LON + LAT, pairs)


def halo_of_two(stack, north_pole, south_pole):
    lats, lons = lax.axis_size(LAT), lax.axis_size(LON)
    rows, cols = stack.shape[1:3]
    odd_row = lax.axis_index(LAT) % 2 == 1
    odd_col = lax.axis_index(LON) % 2 == 1

    def across_chips(i, j):
        to = i + 1 if i % 2 else i - 1
        return (to, j) if 0 <= to < lats else (i, j + lons // 2)

    top, bottom = stack[:, :2], stack[:, rows - 2 :]
    outer = swap(jnp.where(odd_row, bottom, top), across_chips)
    inner = swap(jnp.where(odd_row, top, bottom), lambda i, j: (i - 1 if i % 2 else i + 1, j))
    outer = jnp.where(north_pole | south_pole, outer[:, ::-1], outer)
    above = jnp.where(odd_row, inner, outer)
    below = jnp.where(odd_row, outer, inner)
    tall = jnp.concatenate([above, stack, below], axis=1)
    first, last = tall[:, :, :2], tall[:, :, cols - 2 :]
    far = swap(jnp.where(odd_col, last, first), lambda i, j: (i, j + 1 if j % 2 else j - 1))
    near = swap(jnp.where(odd_col, first, last), lambda i, j: (i, j - 1 if j % 2 else j + 1))
    left = jnp.where(odd_col, near, far)
    right = jnp.where(odd_col, far, near)
    return jnp.concatenate([left, tall, right], axis=2)


def tap_patches(padded):
    row_count, col_count = padded.shape[0] - 2, padded.shape[1] - 2
    return jnp.concatenate(
        [
            padded[tap_row : tap_row + row_count, tap_col : tap_col + col_count]
            for tap_row in range(3)
            for tap_col in range(3)
        ],
        axis=-1,
    )


def apply_kernel(patches, weight):
    return jnp.einsum(
        "rlk,kd->rld", patches, weight.reshape(-1, weight.shape[-1]), preferred_element_type=jnp.float32
    )


def outer_sums(patches, upstream):
    return jnp.einsum("rlk,rld->kd", patches, upstream, preferred_element_type=jnp.float32)


def turned(weight):
    return jnp.transpose(weight[::-1, ::-1], (0, 1, 3, 2))


def adjoint_rows(patches, weight, edge_rows, north_pole, south_pole):
    flipped = turned(weight)
    top = jnp.concatenate([jnp.where(north_pole, flipped[2:3], flipped[0:1]), flipped[1:]])
    bottom = jnp.concatenate([flipped[:2], jnp.where(south_pole, flipped[0:1], flipped[2:3])])
    return jnp.concatenate(
        [
            apply_kernel(patches[:edge_rows], top),
            apply_kernel(patches[edge_rows:-edge_rows], flipped),
            apply_kernel(patches[-edge_rows:], bottom),
        ]
    )


def all_sum(grad_first, grad_second):
    def exchange(v, axes):
        return lax.all_to_all(v, axes, 0, 0, tiled=True)

    def to_all(v, axes):
        return exchange(jnp.broadcast_to(v[None], (lax.axis_size(axes),) + v.shape), axes)

    def other_core(v):
        return lax.ppermute(v, "core", [(0, 1), (1, 0)])

    rows, channels = grad_first.shape
    low_core = lax.axis_index("core") == 0
    kept = jnp.where(low_core, grad_first, grad_second)
    given = jnp.where(low_core, grad_second, grad_first)
    piece = (kept + other_core(given)).astype(jnp.bfloat16)
    size = lax.axis_size(SCATTER)
    piece = jnp.pad(piece, ((0, -rows % (8 * size)), (0, 0))).reshape(size, -1, channels)
    piece = jnp.sum(exchange(piece, SCATTER).astype(jnp.float32), axis=0)
    piece = jnp.sum(to_all(piece, EXCHANGE), axis=0).astype(jnp.bfloat16)
    half = to_all(piece, SCATTER).reshape(-1, channels)[:rows]
    rest = other_core(half)
    first = jnp.where(low_core, half, rest)
    second = jnp.where(low_core, rest, half)
    return first.astype(jnp.float32), second.astype(jnp.float32)


def per_device(fields, cotangent, weight_first, weight_second):
    row_count, col_count, _ = fields.shape
    lat_place = lax.axis_index(LAT)
    north_pole = lat_place == 0
    south_pole = lat_place == lax.axis_size(LAT) - 1
    extended = halo_of_two(jnp.stack([fields, cotangent]), north_pole, south_pole)

    patches_fields = tap_patches(extended[0])
    reversed_first = weight_first[::-1]
    first_sum = jnp.concatenate(
        [
            apply_kernel(patches_fields[:1], jnp.where(north_pole, reversed_first, weight_first)),
            apply_kernel(patches_fields[1:-1], weight_first),
            apply_kernel(patches_fields[-1:], jnp.where(south_pole, reversed_first, weight_first)),
        ]
    )
    hidden = jax.nn.silu(first_sum).astype(jnp.bfloat16)
    back_hidden = adjoint_rows(tap_patches(extended[1]), weight_second, 2, north_pole, south_pole)
    sigmoid_first = jax.nn.sigmoid(first_sum)
    back_first = (back_hidden * sigmoid_first * (1.0 + first_sum * (1.0 - sigmoid_first))).astype(
        jnp.bfloat16
    )
    patches_hidden = tap_patches(hidden)
    cells_total = row_count * lax.axis_size(LAT) * col_count * lax.axis_size(LON)
    grad_scale = 1.0 / math.sqrt(cells_total)
    grad_first = outer_sums(patches_fields[1:-1, 1:-1], back_first[1:-1, 1:-1])
    grad_second = outer_sums(patches_hidden, cotangent)
    grad_first, grad_second = (
        (total * grad_scale).reshape(weight_first.shape) for total in all_sum(grad_first, grad_second)
    )
    second_sum = apply_kernel(patches_hidden, weight_second)
    output = (fields.astype(jnp.float32) + second_sum).astype(jnp.bfloat16)
    back_fields = (
        cotangent.astype(jnp.float32)
        + adjoint_rows(tap_patches(back_first), weight_first, 1, north_pole, south_pole)
    ).astype(jnp.bfloat16)
    return (output, back_fields, grad_first, grad_second)


def solution(mesh):
    fine = Mesh(mesh.devices.reshape(tuple(SIZES.values())), tuple(SIZES))
    cells = P(LAT, LON, None)
    return jax.shard_map(
        per_device,
        mesh=fine,
        in_specs=(cells, cells, P(), P()),
        out_specs=(cells, cells, P(), P()),
        check_vma=False,
    )
```

```python
import math

import jax
import jax.numpy as jnp
from jax import lax
from jax.experimental import pallas as pl
from jax.experimental.pallas import tpu as pltpu
from jax.sharding import Mesh, PartitionSpec as P


LON = ("zh", "y")
LAT = ("x", "zl", "core")
SIZES = {"zh": 4, "y": 8, "x": 4, "zl": 3, "core": 2}
SCATTER = ("y", "x")
EXCHANGE = ("zh", "zl")


def swap(x, partner):
    lats, lons = lax.axis_size(LAT), lax.axis_size(LON)
    pairs = []
    for j in range(lons):
        for i in range(lats):
            to_lat, to_lon = partner(i, j)
            pairs.append((j * lats + i, (to_lon % lons) * lats + to_lat))
    return lax.ppermute(x, LON + LAT, pairs)


def halo_of_two(stack, north_pole, south_pole):
    lats, lons = lax.axis_size(LAT), lax.axis_size(LON)
    rows, cols = stack.shape[1:3]
    odd_row = lax.axis_index(LAT) % 2 == 1
    odd_col = lax.axis_index(LON) % 2 == 1

    def across_chips(i, j):
        to = i + 1 if i % 2 else i - 1
        return (to, j) if 0 <= to < lats else (i, j + lons // 2)

    top, bottom = stack[:, :2], stack[:, rows - 2 :]
    outer = swap(jnp.where(odd_row, bottom, top), across_chips)
    inner = swap(jnp.where(odd_row, top, bottom), lambda i, j: (i - 1 if i % 2 else i + 1, j))
    outer = jnp.where(north_pole | south_pole, outer[:, ::-1], outer)
    above = jnp.where(odd_row, inner, outer)
    below = jnp.where(odd_row, outer, inner)
    tall = jnp.concatenate([above, stack, below], axis=1)
    first, last = tall[:, :, :2], tall[:, :, cols - 2 :]
    far = swap(jnp.where(odd_col, last, first), lambda i, j: (i, j + 1 if j % 2 else j - 1))
    near = swap(jnp.where(odd_col, first, last), lambda i, j: (i, j - 1 if j % 2 else j + 1))
    left = jnp.where(odd_col, near, far).astype(jnp.float32)
    right = jnp.where(odd_col, far, near).astype(jnp.float32)
    return above, below, left, right


def conv_rows(taps_ref, start, count, weight_ref, order):
    total = None
    for tap_row, kernel_row in enumerate(order):
        taps = taps_ref[start + tap_row : start + tap_row + count]
        term = jnp.dot(
            taps.reshape(-1, taps.shape[-1]),
            weight_ref[kernel_row],
            preferred_element_type=jnp.float32,
        )
        total = term if total is None else total + term
    return total.reshape(count, -1, total.shape[-1])


def outer_rows(taps_ref, tap_row, rows, upstream):
    taps = taps_ref[tap_row : tap_row + rows]
    return lax.dot_general(
        taps.reshape(-1, taps.shape[-1]),
        upstream,
        (((0,), (0,)), ((), ())),
        preferred_element_type=jnp.float32,
    )


def ring_kernel(
    flags, fields, cotangent, above, below, left, right, first, turned_second,
    ring, kept, given,
    padded, taps, sums, gates, hidden_taps, field_taps,
):
    rows, cols, channels = fields.shape
    wide = ring.shape[2]
    north, south, low = flags[0] == 1, flags[1] == 1, flags[2] == 1
    for which, own in enumerate((fields, cotangent)):
        padded[which, :, cols:] = jnp.zeros((rows + 4, padded.shape[2] - cols, channels), jnp.float32)
        padded[which, :2, 8 : 8 + cols] = above[which].astype(jnp.float32)
        padded[which, 2 : 2 + rows, 8 : 8 + cols] = own[...].astype(jnp.float32)
        padded[which, 2 + rows :, 8 : 8 + cols] = below[which].astype(jnp.float32)
        padded[which, :, 6:8] = left[which]
        padded[which, :, 8 + cols : 10 + cols] = right[which]
        for tap in range(3):
            taps[which, :, :, channels * tap : channels * (tap + 1)] = padded[
                which, :, 6 + tap : 6 + tap + wide
            ].astype(jnp.bfloat16)
    for tap in range(3):
        field_taps[:, :, channels * tap : channels * (tap + 1)] = padded[
            0, 1 : 3 + rows, 7 + tap : 7 + tap + cols
        ].astype(jnp.bfloat16)
    of_fields, of_cotangent = taps.at[0], taps.at[1]
    sums[0] = conv_rows(of_fields, 0, rows + 2, first, (0, 1, 2))
    sums[1] = conv_rows(of_cotangent, 0, rows + 2, turned_second, (0, 1, 2))

    @pl.when(north)
    def _():
        sums[0, :1] = conv_rows(of_fields, 0, 1, first, (2, 1, 0))
        sums[1, :2] = conv_rows(of_cotangent, 0, 2, turned_second, (2, 1, 2))

    @pl.when(south)
    def _():
        sums[0, rows + 1 :] = conv_rows(of_fields, rows + 1, 1, first, (2, 1, 0))
        sums[1, rows:] = conv_rows(of_cotangent, rows, 2, turned_second, (0, 1, 0))

    first_sum = sums[0]
    gate = jax.nn.sigmoid(first_sum)
    hidden = first_sum * gate
    back_first = sums[1] * gate * (1.0 + first_sum * (1.0 - gate))
    gates[0] = hidden
    gates[1] = back_first
    ring[0] = hidden.astype(jnp.bfloat16)
    ring[1] = back_first.astype(jnp.bfloat16)
    for tap in range(3):
        hidden_taps[:, :, channels * tap : channels * (tap + 1)] = gates[
            0, :, tap : tap + cols
        ].astype(jnp.bfloat16)
    own_back = gates[1, 1 : 1 + rows, 1 : 1 + cols].astype(jnp.bfloat16).reshape(-1, channels)
    own_cotangent = cotangent[...].reshape(-1, channels)
    spare = kept.shape[0] - 9 * channels
    if spare:
        kept[9 * channels :] = jnp.zeros((spare, channels), jnp.float32)
        given[9 * channels :] = jnp.zeros((spare, channels), jnp.float32)
    for tap_row in range(3):
        grad_first = outer_rows(field_taps, tap_row, rows, own_back)
        grad_second = outer_rows(hidden_taps, tap_row, rows, own_cotangent)
        place = slice(3 * channels * tap_row, 3 * channels * (tap_row + 1))

        @pl.when(low)
        def _():
            kept[place] = grad_first
            given[place] = grad_second

        @pl.when(jnp.logical_not(low))
        def _():
            kept[place] = grad_second
            given[place] = grad_first


def output_kernel(flags, ring, fields, cotangent, second, turned_first, output, back_fields, wide_ring, taps, sums):
    rows, cols, channels = fields.shape
    north, south = flags[0] == 1, flags[1] == 1
    for which in range(2):
        wide_ring[which] = ring[which].astype(jnp.float32)
        for tap in range(3):
            taps[which, :, :, channels * tap : channels * (tap + 1)] = wide_ring[
                which, :, tap : tap + cols
            ].astype(jnp.bfloat16)
    second_sum = conv_rows(taps.at[0], 0, rows, second, (0, 1, 2))
    output[...] = (fields[...].astype(jnp.float32) + second_sum).astype(jnp.bfloat16)
    of_back = taps.at[1]
    sums[...] = conv_rows(of_back, 0, rows, turned_first, (0, 1, 2))

    @pl.when(north)
    def _():
        sums[:1] = conv_rows(of_back, 0, 1, turned_first, (2, 1, 2))

    @pl.when(south)
    def _():
        sums[rows - 1 :] = conv_rows(of_back, rows - 1, 1, turned_first, (0, 1, 0))

    back_fields[...] = (cotangent[...].astype(jnp.float32) + sums[...]).astype(jnp.bfloat16)


def call(kernel, out_shapes, scratch, flops, *operands):
    vmem = pl.BlockSpec(memory_space=pltpu.VMEM)
    moved = sum(math.prod(v.shape) * v.dtype.itemsize for v in (*operands, *out_shapes))
    return pl.pallas_call(
        kernel,
        out_shape=out_shapes,
        in_specs=[pl.BlockSpec(memory_space=pltpu.SMEM)] + [vmem] * (len(operands) - 1),
        out_specs=[vmem] * len(out_shapes),
        scratch_shapes=[pltpu.VMEM(shape, dtype) for shape, dtype in scratch],
        compiler_params=pltpu.CompilerParams(vmem_limit_bytes=24 * 2**20),
        cost_estimate=pl.CostEstimate(flops=flops, bytes_accessed=moved, transcendentals=0),
    )(*operands)


def turned(weight):
    return jnp.transpose(weight[::-1, ::-1], (0, 1, 3, 2))


def by_row(weight):
    return weight.reshape(weight.shape[0], -1, weight.shape[-1])


def all_sum(kept, given, finish, operands):
    def exchange(v, axes):
        return lax.all_to_all(v, axes, 0, 0, tiled=True)

    def to_all(v, axes):
        return exchange(jnp.broadcast_to(v[None], (lax.axis_size(axes),) + v.shape), axes)

    def other_core(v):
        return lax.ppermute(v, "core", [(0, 1), (1, 0)])

    channels = kept.shape[-1]
    piece = (kept + other_core(given)).astype(jnp.bfloat16)
    piece, operands = lax.optimization_barrier((piece, operands))
    outputs = finish(*operands)
    piece = piece.reshape(lax.axis_size(SCATTER), -1, channels)
    piece = jnp.sum(exchange(piece, SCATTER).astype(jnp.float32), axis=0)
    piece = jnp.sum(to_all(piece, EXCHANGE), axis=0).astype(jnp.bfloat16)
    half = to_all(piece, SCATTER).reshape(-1, channels)[: 9 * channels]
    half, outputs = lax.optimization_barrier((half, outputs))
    return half, other_core(half), outputs


def per_device(fields, cotangent, weight_first, weight_second):
    rows, cols, channels = fields.shape
    lat_place = lax.axis_index(LAT)
    north_pole = lat_place == 0
    south_pole = lat_place == lax.axis_size(LAT) - 1
    low_core = lax.axis_index("core") == 0
    flags = jnp.stack([north_pole, south_pole, low_core, low_core]).astype(jnp.int32)
    edges = halo_of_two(jnp.stack([fields, cotangent]), north_pole, south_pole)
    wide = -(-(cols + 2) // 16) * 16
    taps = 3 * channels
    flops = 2 * rows * cols * channels * channels * 9
    split = 8 * lax.axis_size(SCATTER)
    half = jax.ShapeDtypeStruct((-(-9 * channels // split) * split, channels), jnp.float32)
    bf16, f32 = jnp.bfloat16, jnp.float32
    ring, kept, given = call(
        ring_kernel,
        (jax.ShapeDtypeStruct((2, rows + 2, wide, channels), bf16), half, half),
        (
            ((2, rows + 4, wide + 8, channels), f32),
            ((2, rows + 4, wide, taps), bf16),
            ((2, rows + 2, wide, channels), f32),
            ((2, rows + 2, wide, channels), f32),
            ((rows + 2, cols, taps), bf16),
            ((rows + 2, cols, taps), bf16),
        ),
        4 * flops,
        flags, fields, cotangent, *edges, by_row(weight_first), by_row(turned(weight_second)),
    )
    block = jax.ShapeDtypeStruct(fields.shape, bf16)

    def finish(*operands):
        return call(
            output_kernel,
            (block, block),
            (
                ((2, rows + 2, wide, channels), f32),
                ((2, rows + 2, cols, taps), bf16),
                ((rows, cols, channels), f32),
            ),
            2 * flops,
            *operands,
        )

    mine, theirs, (output, back_fields) = all_sum(
        kept,
        given,
        finish,
        (flags, ring, fields, cotangent, by_row(weight_second), by_row(turned(weight_first))),
    )
    cells_total = rows * lax.axis_size(LAT) * cols * lax.axis_size(LON)
    grad_scale = 1.0 / math.sqrt(cells_total)
    grad_first, grad_second = (
        (jnp.where(low_core, one, other).astype(f32) * grad_scale).reshape(weight_first.shape)
        for one, other in ((mine, theirs), (theirs, mine))
    )
    return (output, back_fields, grad_first, grad_second)


def solution(mesh):
    fine = Mesh(mesh.devices.reshape(tuple(SIZES.values())), tuple(SIZES))
    cells = P(LAT, LON, None)
    return jax.shard_map(
        per_device,
        mesh=fine,
        in_specs=(cells, cells, P(), P()),
        out_specs=(cells, cells, P(), P()),
        check_vma=False,
    )
```

```python
import math

import jax
import jax.numpy as jnp
from jax import lax
from jax.experimental import pallas as pl
from jax.experimental.pallas import tpu as pltpu
from jax.sharding import Mesh, PartitionSpec as P


LON = ("zh", "y")
LAT = ("x", "zl", "core")
SIZES = {"zh": 4, "y": 8, "x": 4, "zl": 3, "core": 2}
SCATTER = ("y", "x")
EXCHANGE = ("zh", "zl")


def swap(x, partner):
    lats, lons = lax.axis_size(LAT), lax.axis_size(LON)
    pairs = []
    for j in range(lons):
        for i in range(lats):
            to_lat, to_lon = partner(i, j)
            pairs.append((j * lats + i, (to_lon % lons) * lats + to_lat))
    return lax.ppermute(x, LON + LAT, pairs)


def halo_of_two(stack, north_pole, south_pole):
    lats, lons = lax.axis_size(LAT), lax.axis_size(LON)
    rows, cols = stack.shape[1:3]
    odd_row = lax.axis_index(LAT) % 2 == 1
    odd_col = lax.axis_index(LON) % 2 == 1

    def across_chips(i, j):
        to = i + 1 if i % 2 else i - 1
        return (to, j) if 0 <= to < lats else (i, j + lons // 2)

    top, bottom = stack[:, :2], stack[:, rows - 2 :]
    outer = swap(jnp.where(odd_row, bottom, top), across_chips)
    inner = swap(jnp.where(odd_row, top, bottom), lambda i, j: (i - 1 if i % 2 else i + 1, j))
    outer = jnp.where(north_pole | south_pole, outer[:, ::-1], outer)
    above = jnp.where(odd_row, inner, outer)
    below = jnp.where(odd_row, outer, inner)
    tall = jnp.concatenate([above, stack, below], axis=1)
    first, last = tall[:, :, :2], tall[:, :, cols - 2 :]
    far = swap(jnp.where(odd_col, last, first), lambda i, j: (i, j + 1 if j % 2 else j - 1))
    near = swap(jnp.where(odd_col, first, last), lambda i, j: (i, j - 1 if j % 2 else j + 1))
    left = jnp.where(odd_col, near, far).astype(jnp.float32)
    right = jnp.where(odd_col, far, near).astype(jnp.float32)
    return above, below, left, right


def conv_rows(taps_ref, start, count, weight_ref, order):
    total = None
    for tap_row, kernel_row in enumerate(order):
        taps = taps_ref[start + tap_row : start + tap_row + count]
        term = jnp.dot(
            taps.reshape(-1, taps.shape[-1]),
            weight_ref[kernel_row],
            preferred_element_type=jnp.float32,
        )
        total = term if total is None else total + term
    return total.reshape(count, -1, total.shape[-1])


def outer_rows(taps_ref, tap_row, rows, upstream):
    taps = taps_ref[tap_row : tap_row + rows]
    return lax.dot_general(
        taps.reshape(-1, taps.shape[-1]),
        upstream,
        (((0,), (0,)), ((), ())),
        preferred_element_type=jnp.float32,
    )


def ring_kernel(
    flags, fields, cotangent, above, below, left, right, first, turned_second,
    ring, kept, given,
    padded, taps, sums, gates, hidden_taps, field_taps,
):
    rows, cols, channels = fields.shape
    wide = ring.shape[2]
    north, south, low = flags[0] == 1, flags[1] == 1, flags[2] == 1
    for which, own in enumerate((fields, cotangent)):
        padded[which, :, cols:] = jnp.zeros((rows + 4, padded.shape[2] - cols, channels), jnp.float32)
        padded[which, :2, 8 : 8 + cols] = above[which].astype(jnp.float32)
        padded[which, 2 : 2 + rows, 8 : 8 + cols] = own[...].astype(jnp.float32)
        padded[which, 2 + rows :, 8 : 8 + cols] = below[which].astype(jnp.float32)
        padded[which, :, 6:8] = left[which]
        padded[which, :, 8 + cols : 10 + cols] = right[which]
        for tap in range(3):
            taps[which, :, :, channels * tap : channels * (tap + 1)] = padded[
                which, :, 6 + tap : 6 + tap + wide
            ].astype(jnp.bfloat16)
    for tap in range(3):
        field_taps[:, :, channels * tap : channels * (tap + 1)] = padded[
            0, 1 : 3 + rows, 7 + tap : 7 + tap + cols
        ].astype(jnp.bfloat16)
    of_fields, of_cotangent = taps.at[0], taps.at[1]
    sums[0] = conv_rows(of_fields, 0, rows + 2, first, (0, 1, 2))
    sums[1] = conv_rows(of_cotangent, 0, rows + 2, turned_second, (0, 1, 2))

    @pl.when(north)
    def _():
        sums[0, :1] = conv_rows(of_fields, 0, 1, first, (2, 1, 0))
        sums[1, :2] = conv_rows(of_cotangent, 0, 2, turned_second, (2, 1, 2))

    @pl.when(south)
    def _():
        sums[0, rows + 1 :] = conv_rows(of_fields, rows + 1, 1, first, (2, 1, 0))
        sums[1, rows:] = conv_rows(of_cotangent, rows, 2, turned_second, (0, 1, 0))

    first_sum = sums[0]
    gate = jax.nn.sigmoid(first_sum)
    hidden = first_sum * gate
    back_first = sums[1] * gate * (1.0 + first_sum * (1.0 - gate))
    gates[0] = hidden
    gates[1] = back_first
    ring[0] = hidden.astype(jnp.bfloat16)
    ring[1] = back_first.astype(jnp.bfloat16)
    for tap in range(3):
        hidden_taps[:, :, channels * tap : channels * (tap + 1)] = gates[
            0, :, tap : tap + cols
        ].astype(jnp.bfloat16)
    own_back = gates[1, 1 : 1 + rows, 1 : 1 + cols].astype(jnp.bfloat16).reshape(-1, channels)
    own_cotangent = cotangent[...].reshape(-1, channels)
    for tap_row in range(3):
        grad_first = outer_rows(field_taps, tap_row, rows, own_back)
        grad_second = outer_rows(hidden_taps, tap_row, rows, own_cotangent)
        place = slice(3 * channels * tap_row, 3 * channels * (tap_row + 1))

        @pl.when(low)
        def _():
            kept[place] = grad_first
            given[place] = grad_second

        @pl.when(jnp.logical_not(low))
        def _():
            kept[place] = grad_second
            given[place] = grad_first


def output_kernel(flags, ring, fields, cotangent, second, turned_first, output, back_fields, wide_ring, taps, sums):
    rows, cols, channels = fields.shape
    north, south = flags[0] == 1, flags[1] == 1
    for which in range(2):
        wide_ring[which] = ring[which].astype(jnp.float32)
        for tap in range(3):
            taps[which, :, :, channels * tap : channels * (tap + 1)] = wide_ring[
                which, :, tap : tap + cols
            ].astype(jnp.bfloat16)
    second_sum = conv_rows(taps.at[0], 0, rows, second, (0, 1, 2))
    output[...] = (fields[...].astype(jnp.float32) + second_sum).astype(jnp.bfloat16)
    of_back = taps.at[1]
    sums[...] = conv_rows(of_back, 0, rows, turned_first, (0, 1, 2))

    @pl.when(north)
    def _():
        sums[:1] = conv_rows(of_back, 0, 1, turned_first, (2, 1, 2))

    @pl.when(south)
    def _():
        sums[rows - 1 :] = conv_rows(of_back, rows - 1, 1, turned_first, (0, 1, 0))

    back_fields[...] = (cotangent[...].astype(jnp.float32) + sums[...]).astype(jnp.bfloat16)


def call(kernel, out_shapes, scratch, flops, *operands):
    vmem = pl.BlockSpec(memory_space=pltpu.VMEM)
    moved = sum(math.prod(v.shape) * v.dtype.itemsize for v in (*operands, *out_shapes))
    return pl.pallas_call(
        kernel,
        out_shape=out_shapes,
        in_specs=[pl.BlockSpec(memory_space=pltpu.SMEM)] + [vmem] * (len(operands) - 1),
        out_specs=[vmem] * len(out_shapes),
        scratch_shapes=[pltpu.VMEM(shape, dtype) for shape, dtype in scratch],
        compiler_params=pltpu.CompilerParams(vmem_limit_bytes=24 * 2**20),
        cost_estimate=pl.CostEstimate(flops=flops, bytes_accessed=moved, transcendentals=0),
    )(*operands)


def turned(weight):
    return jnp.transpose(weight[::-1, ::-1], (0, 1, 3, 2))


def by_row(weight):
    return weight.reshape(weight.shape[0], -1, weight.shape[-1])


def all_sum(kept, given, finish, operands):
    def exchange(v, axes):
        return lax.all_to_all(v, axes, 0, 0, tiled=True)

    def to_all(v, axes):
        return exchange(jnp.broadcast_to(v[None], (lax.axis_size(axes),) + v.shape), axes)

    def total(v):
        return jnp.sum(v.astype(jnp.float32), axis=0).astype(jnp.bfloat16)

    def other_core(v):
        return lax.ppermute(v, "core", [(0, 1), (1, 0)])

    channels = kept.shape[-1]
    piece = (kept + other_core(given)).astype(jnp.bfloat16)
    piece, operands = lax.optimization_barrier((piece, operands))
    outputs = finish(*operands)
    piece = piece.reshape(lax.axis_size(SCATTER), -1, 4, channels)
    piece = total(exchange(piece, SCATTER))
    piece = total(to_all(piece, EXCHANGE))
    half = to_all(piece, SCATTER).reshape(-1, channels)
    half, outputs = lax.optimization_barrier((half, outputs))
    return half, other_core(half), outputs


def per_device(fields, cotangent, weight_first, weight_second):
    rows, cols, channels = fields.shape
    lat_place = lax.axis_index(LAT)
    north_pole = lat_place == 0
    south_pole = lat_place == lax.axis_size(LAT) - 1
    low_core = lax.axis_index("core") == 0
    flags = jnp.stack([north_pole, south_pole, low_core, low_core]).astype(jnp.int32)
    edges = halo_of_two(jnp.stack([fields, cotangent]), north_pole, south_pole)
    wide = -(-(cols + 2) // 16) * 16
    taps = 3 * channels
    flops = 2 * rows * cols * channels * channels * 9
    half = jax.ShapeDtypeStruct((9 * channels, channels), jnp.float32)
    bf16, f32 = jnp.bfloat16, jnp.float32
    ring, kept, given = call(
        ring_kernel,
        (jax.ShapeDtypeStruct((2, rows + 2, wide, channels), bf16), half, half),
        (
            ((2, rows + 4, wide + 8, channels), f32),
            ((2, rows + 4, wide, taps), bf16),
            ((2, rows + 2, wide, channels), f32),
            ((2, rows + 2, wide, channels), f32),
            ((rows + 2, cols, taps), bf16),
            ((rows + 2, cols, taps), bf16),
        ),
        4 * flops,
        flags, fields, cotangent, *edges, by_row(weight_first), by_row(turned(weight_second)),
    )
    block = jax.ShapeDtypeStruct(fields.shape, bf16)

    def finish(*operands):
        return call(
            output_kernel,
            (block, block),
            (
                ((2, rows + 2, wide, channels), f32),
                ((2, rows + 2, cols, taps), bf16),
                ((rows, cols, channels), f32),
            ),
            2 * flops,
            *operands,
        )

    mine, theirs, (output, back_fields) = all_sum(
        kept,
        given,
        finish,
        (flags, ring, fields, cotangent, by_row(weight_second), by_row(turned(weight_first))),
    )
    cells_total = rows * lax.axis_size(LAT) * cols * lax.axis_size(LON)
    grad_scale = 1.0 / math.sqrt(cells_total)
    grad_first, grad_second = (
        (jnp.where(low_core, one, other).astype(f32) * grad_scale).reshape(weight_first.shape)
        for one, other in ((mine, theirs), (theirs, mine))
    )
    return (output, back_fields, grad_first, grad_second)


def solution(mesh):
    fine = Mesh(mesh.devices.reshape(tuple(SIZES.values())), tuple(SIZES))
    cells = P(LAT, LON, None)
    return jax.shard_map(
        per_device,
        mesh=fine,
        in_specs=(cells, cells, P(), P()),
        out_specs=(cells, cells, P(), P()),
        check_vma=False,
    )
```

```python
import math

import jax
import jax.numpy as jnp
from jax import lax
from jax.experimental import pallas as pl
from jax.experimental.pallas import tpu as pltpu
from jax.sharding import Mesh, PartitionSpec as P


LON = ("zh", "y")
LAT = ("x", "zl", "core")
SIZES = {"zh": 4, "y": 8, "x": 4, "zl": 3, "core": 2}
SCATTER = ("y", "x")
EXCHANGE = ("zh", "zl")


def swap(x, partner):
    lats, lons = lax.axis_size(LAT), lax.axis_size(LON)
    pairs = []
    for j in range(lons):
        for i in range(lats):
            to_lat, to_lon = partner(i, j)
            pairs.append((j * lats + i, (to_lon % lons) * lats + to_lat))
    return lax.ppermute(x, LON + LAT, pairs)


def halo_of_two(stack, north_pole, south_pole):
    lats, lons = lax.axis_size(LAT), lax.axis_size(LON)
    rows, cols = stack.shape[1:3]
    odd_row = lax.axis_index(LAT) % 2 == 1
    odd_col = lax.axis_index(LON) % 2 == 1

    def across_chips(i, j):
        to = i + 1 if i % 2 else i - 1
        return (to, j) if 0 <= to < lats else (i, j + lons // 2)

    top, bottom = stack[:, :2], stack[:, rows - 2 :]
    outer = swap(jnp.where(odd_row, bottom, top), across_chips)
    inner = swap(jnp.where(odd_row, top, bottom), lambda i, j: (i - 1 if i % 2 else i + 1, j))
    outer = jnp.where(north_pole | south_pole, outer[:, ::-1], outer)
    above = jnp.where(odd_row, inner, outer)
    below = jnp.where(odd_row, outer, inner)
    tall = jnp.concatenate([above, stack, below], axis=1)
    first, last = tall[:, :, :2], tall[:, :, cols - 2 :]
    far = swap(jnp.where(odd_col, last, first), lambda i, j: (i, j + 1 if j % 2 else j - 1))
    near = swap(jnp.where(odd_col, first, last), lambda i, j: (i, j - 1 if j % 2 else j + 1))
    left = jnp.where(odd_col, near, far).astype(jnp.float32)
    right = jnp.where(odd_col, far, near).astype(jnp.float32)
    return above, below, left, right


def conv_rows(taps_ref, start, count, weight_ref, order):
    total = None
    for tap_row, kernel_row in enumerate(order):
        taps = taps_ref[start + tap_row : start + tap_row + count]
        term = jnp.dot(
            taps.reshape(-1, taps.shape[-1]),
            weight_ref[kernel_row],
            preferred_element_type=jnp.float32,
        )
        total = term if total is None else total + term
    return total.reshape(count, -1, total.shape[-1])


def conv_pairs(taps_ref, pairs, weight_ref):
    zero = jnp.zeros(weight_ref.shape[1:], weight_ref.dtype)
    depth, channels = weight_ref.shape[0], weight_ref.shape[-1]
    total = None
    for start in range(0, depth + 1, 2):
        taps = jnp.concatenate(
            [
                jnp.concatenate([taps_ref[2 * pair + start + step] for pair in range(pairs)], axis=0)
                for step in range(2)
            ],
            axis=1,
        )
        weight = jnp.concatenate(
            [
                jnp.concatenate(
                    [
                        weight_ref[row - out] if 0 <= row - out < depth else zero
                        for out in range(2)
                    ],
                    axis=1,
                )
                for row in (start, start + 1)
            ],
            axis=0,
        )
        term = jnp.dot(taps, weight, preferred_element_type=jnp.float32)
        total = term if total is None else total + term
    total = total.reshape(pairs, -1, 2 * channels)
    return total[:, :, :channels], total[:, :, channels:]


def outer_rows(taps_ref, tap_row, rows, upstream_turned):
    taps = taps_ref[tap_row : tap_row + rows]
    return jnp.dot(
        upstream_turned, taps.reshape(-1, taps.shape[-1]), preferred_element_type=jnp.float32
    ).T


def ring_kernel(
    flags, fields, cotangent, above, below, left, right, first, turned_second,
    ring, kept, given,
    padded, taps, sums, gates, hidden_taps, field_taps,
):
    rows, cols, channels = fields.shape
    wide = ring.shape[2]
    north, south, low = flags[0] == 1, flags[1] == 1, flags[2] == 1
    for which, own in enumerate((fields, cotangent)):
        padded[which, :, cols:] = jnp.zeros((rows + 4, padded.shape[2] - cols, channels), jnp.float32)
        padded[which, :2, 8 : 8 + cols] = above[which].astype(jnp.float32)
        padded[which, 2 : 2 + rows, 8 : 8 + cols] = own[...].astype(jnp.float32)
        padded[which, 2 + rows :, 8 : 8 + cols] = below[which].astype(jnp.float32)
        padded[which, :, 6:8] = left[which]
        padded[which, :, 8 + cols : 10 + cols] = right[which]
        for tap in range(3):
            taps[which, :, :, channels * tap : channels * (tap + 1)] = padded[
                which, :, 6 + tap : 6 + tap + wide
            ].astype(jnp.bfloat16)
    for tap in range(3):
        field_taps[:, :, channels * tap : channels * (tap + 1)] = padded[
            0, 1 : 3 + rows, 7 + tap : 7 + tap + cols
        ].astype(jnp.bfloat16)
    of_fields, of_cotangent = taps.at[0], taps.at[1]
    pairs = (rows + 2) // 2
    for which, weight in enumerate((first, turned_second)):
        for out, part in enumerate(conv_pairs(taps.at[which], pairs, weight)):
            for pair in range(pairs):
                sums[which, 2 * pair + out] = part[pair]

    @pl.when(north)
    def _():
        sums[0, :1] = conv_rows(of_fields, 0, 1, first, (2, 1, 0))
        sums[1, :2] = conv_rows(of_cotangent, 0, 2, turned_second, (2, 1, 2))

    @pl.when(south)
    def _():
        sums[0, rows + 1 :] = conv_rows(of_fields, rows + 1, 1, first, (2, 1, 0))
        sums[1, rows:] = conv_rows(of_cotangent, rows, 2, turned_second, (0, 1, 0))

    first_sum = sums[0]
    gate = jax.nn.sigmoid(first_sum)
    hidden = first_sum * gate
    back_first = sums[1] * gate * (1.0 + first_sum * (1.0 - gate))
    gates[0] = hidden
    gates[1] = back_first
    ring[0] = hidden.astype(jnp.bfloat16)
    ring[1] = back_first.astype(jnp.bfloat16)
    for tap in range(3):
        hidden_taps[:, :, channels * tap : channels * (tap + 1)] = gates[
            0, :, tap : tap + cols
        ].astype(jnp.bfloat16)
    own_back = gates[1, 1 : 1 + rows, 1 : 1 + cols].astype(jnp.bfloat16).reshape(-1, channels).T
    own_cotangent = cotangent[...].reshape(-1, channels).T
    for tap_row in range(3):
        grad_first = outer_rows(field_taps, tap_row, rows, own_back)
        grad_second = outer_rows(hidden_taps, tap_row, rows, own_cotangent)
        place = slice(3 * channels * tap_row, 3 * channels * (tap_row + 1))
        kept[place] = jnp.where(low, grad_first, grad_second)
        given[place] = jnp.where(low, grad_second, grad_first)


def output_kernel(flags, ring, fields, cotangent, second, turned_first, output, back_fields, wide_ring, taps, sums):
    rows, cols, channels = fields.shape
    north, south = flags[0] == 1, flags[1] == 1
    for which in range(2):
        wide_ring[which] = ring[which].astype(jnp.float32)
        for tap in range(3):
            taps[which, :, :, channels * tap : channels * (tap + 1)] = wide_ring[
                which, :, tap : tap + cols
            ].astype(jnp.bfloat16)
    for out, part in enumerate(conv_pairs(taps.at[0], rows // 2, second)):
        for pair in range(rows // 2):
            row = 2 * pair + out
            output[row] = (fields[row].astype(jnp.float32) + part[pair]).astype(jnp.bfloat16)
    of_back = taps.at[1]
    for out, part in enumerate(conv_pairs(of_back, rows // 2, turned_first)):
        for pair in range(rows // 2):
            sums[2 * pair + out] = part[pair]

    @pl.when(north)
    def _():
        sums[:1] = conv_rows(of_back, 0, 1, turned_first, (2, 1, 2))

    @pl.when(south)
    def _():
        sums[rows - 1 :] = conv_rows(of_back, rows - 1, 1, turned_first, (0, 1, 0))

    back_fields[...] = (cotangent[...].astype(jnp.float32) + sums[...]).astype(jnp.bfloat16)


def call(kernel, out_shapes, scratch, flops, *operands):
    vmem = pl.BlockSpec(memory_space=pltpu.VMEM)
    moved = sum(math.prod(v.shape) * v.dtype.itemsize for v in (*operands, *out_shapes))
    return pl.pallas_call(
        kernel,
        out_shape=out_shapes,
        in_specs=[pl.BlockSpec(memory_space=pltpu.SMEM)] + [vmem] * (len(operands) - 1),
        out_specs=[vmem] * len(out_shapes),
        scratch_shapes=[pltpu.VMEM(shape, dtype) for shape, dtype in scratch],
        compiler_params=pltpu.CompilerParams(vmem_limit_bytes=24 * 2**20),
        cost_estimate=pl.CostEstimate(flops=flops, bytes_accessed=moved, transcendentals=0),
    )(*operands)


def turned(weight):
    return jnp.transpose(weight[::-1, ::-1], (0, 1, 3, 2))


def by_row(weight):
    return weight.reshape(weight.shape[0], -1, weight.shape[-1])


def all_sum(kept, given, finish, operands):
    def exchange(v, axes):
        return lax.all_to_all(v, axes, 0, 0, tiled=True)

    def to_all(v, axes):
        return exchange(jnp.broadcast_to(v[None], (lax.axis_size(axes),) + v.shape), axes)

    def total(v):
        return jnp.sum(v.astype(jnp.float32), axis=0).astype(jnp.bfloat16)

    def other_core(v):
        return lax.ppermute(v, "core", [(0, 1), (1, 0)])

    channels = kept.shape[-1]
    piece = (kept + other_core(given)).astype(jnp.bfloat16)
    piece = piece.reshape(lax.axis_size(SCATTER), -1, 4, channels)
    piece = total(exchange(piece, SCATTER))
    piece = total(to_all(piece, EXCHANGE))
    half = to_all(piece, SCATTER).reshape(-1, channels)
    half, operands = lax.optimization_barrier((half, operands))
    return half, other_core(half), finish(*operands)


def per_device(fields, cotangent, weight_first, weight_second):
    rows, cols, channels = fields.shape
    lat_place = lax.axis_index(LAT)
    north_pole = lat_place == 0
    south_pole = lat_place == lax.axis_size(LAT) - 1
    low_core = lax.axis_index("core") == 0
    flags = jnp.stack([north_pole, south_pole, low_core, low_core]).astype(jnp.int32)
    edges = halo_of_two(jnp.stack([fields, cotangent]), north_pole, south_pole)
    turned_first = by_row(turned(weight_first))
    edges, turned_first = lax.optimization_barrier((edges, turned_first))
    wide = -(-(cols + 2) // 16) * 16
    taps = 3 * channels
    flops = 2 * rows * cols * channels * channels * 9
    half = jax.ShapeDtypeStruct((9 * channels, channels), jnp.float32)
    bf16, f32 = jnp.bfloat16, jnp.float32
    ring, kept, given = call(
        ring_kernel,
        (jax.ShapeDtypeStruct((2, rows + 2, wide, channels), bf16), half, half),
        (
            ((2, rows + 4, wide + 8, channels), f32),
            ((2, rows + 4, wide, taps), bf16),
            ((2, rows + 2, wide, channels), f32),
            ((2, rows + 2, wide, channels), f32),
            ((rows + 2, cols, taps), bf16),
            ((rows + 2, cols, taps), bf16),
        ),
        4 * flops,
        flags, fields, cotangent, *edges, by_row(weight_first), by_row(turned(weight_second)),
    )
    block = jax.ShapeDtypeStruct(fields.shape, bf16)

    def finish(*operands):
        return call(
            output_kernel,
            (block, block),
            (
                ((2, rows + 2, wide, channels), f32),
                ((2, rows + 2, cols, taps), bf16),
                ((rows, cols, channels), f32),
            ),
            2 * flops,
            *operands,
        )

    mine, theirs, (output, back_fields) = all_sum(
        kept,
        given,
        finish,
        (flags, ring, fields, cotangent, by_row(weight_second), turned_first),
    )
    cells_total = rows * lax.axis_size(LAT) * cols * lax.axis_size(LON)
    grad_scale = 1.0 / math.sqrt(cells_total)
    grad_first, grad_second = (
        (jnp.where(low_core, one, other).astype(f32) * grad_scale).reshape(weight_first.shape)
        for one, other in ((mine, theirs), (theirs, mine))
    )
    return (output, back_fields, grad_first, grad_second)


def solution(mesh):
    fine = Mesh(mesh.devices.reshape(tuple(SIZES.values())), tuple(SIZES))
    cells = P(LAT, LON, None)
    return jax.shard_map(
        per_device,
        mesh=fine,
        in_specs=(cells, cells, P(), P()),
        out_specs=(cells, cells, P(), P()),
        check_vma=False,
    )
```

```python
import math

import jax
import jax.numpy as jnp
from jax import lax
from jax.experimental import pallas as pl
from jax.experimental.pallas import tpu as pltpu
from jax.sharding import Mesh, PartitionSpec as P


LON = ("zh", "y")
LAT = ("x", "zl", "core")
SIZES = {"zh": 4, "y": 8, "x": 4, "zl": 3, "core": 2}
SCATTER = ("y", "x")
EXCHANGE = ("zl", "zh")


def swap(x, partner):
    lats, lons = lax.axis_size(LAT), lax.axis_size(LON)
    pairs = []
    for j in range(lons):
        for i in range(lats):
            to_lat, to_lon = partner(i, j)
            pairs.append((j * lats + i, (to_lon % lons) * lats + to_lat))
    return lax.ppermute(x, LON + LAT, pairs)


def halo_of_two(stack, north_pole, south_pole):
    lats, lons = lax.axis_size(LAT), lax.axis_size(LON)
    rows, cols = stack.shape[1:3]
    odd_row = lax.axis_index(LAT) % 2 == 1
    odd_col = lax.axis_index(LON) % 2 == 1

    def across_chips(i, j):
        to = i + 1 if i % 2 else i - 1
        return (to, j) if 0 <= to < lats else (i, j + lons // 2)

    top, bottom = stack[:, :2], stack[:, rows - 2 :]
    outer = swap(jnp.where(odd_row, bottom, top), across_chips)
    inner = swap(jnp.where(odd_row, top, bottom), lambda i, j: (i - 1 if i % 2 else i + 1, j))
    outer = jnp.where(north_pole | south_pole, outer[:, ::-1], outer)
    above = jnp.where(odd_row, inner, outer)
    below = jnp.where(odd_row, outer, inner)
    tall = jnp.concatenate([above, stack, below], axis=1)
    first, last = tall[:, :, :2], tall[:, :, cols - 2 :]
    far = swap(jnp.where(odd_col, last, first), lambda i, j: (i, j + 1 if j % 2 else j - 1))
    near = swap(jnp.where(odd_col, first, last), lambda i, j: (i, j - 1 if j % 2 else j + 1))
    left = jnp.where(odd_col, near, far).astype(jnp.float32)
    right = jnp.where(odd_col, far, near).astype(jnp.float32)
    return above, below, left, right


def conv_rows(taps_ref, start, count, weight_ref, order):
    total = None
    for tap_row, kernel_row in enumerate(order):
        taps = taps_ref[start + tap_row : start + tap_row + count]
        term = jnp.dot(
            taps.reshape(-1, taps.shape[-1]),
            weight_ref[kernel_row],
            preferred_element_type=jnp.float32,
        )
        total = term if total is None else total + term
    return total.reshape(count, -1, total.shape[-1])


def conv_pairs(taps_ref, pairs, weight_ref):
    zero = jnp.zeros(weight_ref.shape[1:], weight_ref.dtype)
    depth, channels = weight_ref.shape[0], weight_ref.shape[-1]
    total = None
    for start in range(0, depth + 1, 2):
        taps = jnp.concatenate(
            [
                jnp.concatenate([taps_ref[2 * pair + start + step] for pair in range(pairs)], axis=0)
                for step in range(2)
            ],
            axis=1,
        )
        weight = jnp.concatenate(
            [
                jnp.concatenate(
                    [
                        weight_ref[row - out] if 0 <= row - out < depth else zero
                        for out in range(2)
                    ],
                    axis=1,
                )
                for row in (start, start + 1)
            ],
            axis=0,
        )
        term = jnp.dot(taps, weight, preferred_element_type=jnp.float32)
        total = term if total is None else total + term
    total = total.reshape(pairs, -1, 2 * channels)
    return total[:, :, :channels], total[:, :, channels:]


def outer_rows(taps_ref, tap_row, rows, upstream_turned):
    taps = taps_ref[tap_row : tap_row + rows]
    return jnp.dot(
        upstream_turned, taps.reshape(-1, taps.shape[-1]), preferred_element_type=jnp.float32
    ).T


def ring_kernel(
    flags, fields, cotangent, above, below, left, right, first, turned_second,
    ring, hidden_taps, kept, given,
    padded, taps, sums, gates, field_taps,
):
    rows, cols, channels = fields.shape
    wide = ring.shape[1]
    north, south, low = flags[0] == 1, flags[1] == 1, flags[2] == 1
    for which, own in enumerate((fields, cotangent)):
        padded[which, :, cols:] = jnp.zeros((rows + 4, padded.shape[2] - cols, channels), jnp.float32)
        padded[which, :2, 8 : 8 + cols] = above[which].astype(jnp.float32)
        padded[which, 2 : 2 + rows, 8 : 8 + cols] = own[...].astype(jnp.float32)
        padded[which, 2 + rows :, 8 : 8 + cols] = below[which].astype(jnp.float32)
        padded[which, :, 6:8] = left[which]
        padded[which, :, 8 + cols : 10 + cols] = right[which]
        for tap in range(3):
            taps[which, :, :, channels * tap : channels * (tap + 1)] = padded[
                which, :, 6 + tap : 6 + tap + wide
            ].astype(jnp.bfloat16)
    for tap in range(3):
        field_taps[:, :, channels * tap : channels * (tap + 1)] = padded[
            0, 1 : 3 + rows, 7 + tap : 7 + tap + cols
        ].astype(jnp.bfloat16)
    of_fields, of_cotangent = taps.at[0], taps.at[1]
    pairs = (rows + 2) // 2
    for which, weight in enumerate((first, turned_second)):
        for out, part in enumerate(conv_pairs(taps.at[which], pairs, weight)):
            for pair in range(pairs):
                sums[which, 2 * pair + out] = part[pair]

    @pl.when(north)
    def _():
        sums[0, :1] = conv_rows(of_fields, 0, 1, first, (2, 1, 0))
        sums[1, :2] = conv_rows(of_cotangent, 0, 2, turned_second, (2, 1, 2))

    @pl.when(south)
    def _():
        sums[0, rows + 1 :] = conv_rows(of_fields, rows + 1, 1, first, (2, 1, 0))
        sums[1, rows:] = conv_rows(of_cotangent, rows, 2, turned_second, (0, 1, 0))

    first_sum = sums[0]
    gate = jax.nn.sigmoid(first_sum)
    hidden = first_sum * gate
    back_first = sums[1] * gate * (1.0 + first_sum * (1.0 - gate))
    gates[0] = hidden
    gates[1] = back_first
    ring[...] = back_first.astype(jnp.bfloat16)
    for tap in range(3):
        hidden_taps[:, :, channels * tap : channels * (tap + 1)] = gates[
            0, :, tap : tap + cols
        ].astype(jnp.bfloat16)
    own_back = gates[1, 1 : 1 + rows, 1 : 1 + cols].astype(jnp.bfloat16).reshape(-1, channels).T
    own_cotangent = cotangent[...].reshape(-1, channels).T
    for tap_row in range(3):
        grad_first = outer_rows(field_taps, tap_row, rows, own_back)
        grad_second = outer_rows(hidden_taps, tap_row, rows, own_cotangent)
        place = slice(3 * channels * tap_row, 3 * channels * (tap_row + 1))
        kept[place] = jnp.where(low, grad_first, grad_second)
        given[place] = jnp.where(low, grad_second, grad_first)


def output_kernel(flags, hidden_taps, fields, second, output):
    rows = fields.shape[0]
    for out, part in enumerate(conv_pairs(hidden_taps, rows // 2, second)):
        for pair in range(rows // 2):
            row = 2 * pair + out
            output[row] = (fields[row].astype(jnp.float32) + part[pair]).astype(jnp.bfloat16)


def back_kernel(flags, ring, cotangent, turned_first, back_fields, wide_ring, taps, sums):
    rows, cols, channels = cotangent.shape
    north, south = flags[0] == 1, flags[1] == 1
    wide_ring[...] = ring[...].astype(jnp.float32)
    for tap in range(3):
        taps[:, :, channels * tap : channels * (tap + 1)] = wide_ring[:, tap : tap + cols].astype(
            jnp.bfloat16
        )
    for out, part in enumerate(conv_pairs(taps, rows // 2, turned_first)):
        for pair in range(rows // 2):
            sums[2 * pair + out] = part[pair]

    @pl.when(north)
    def _():
        sums[:1] = conv_rows(taps, 0, 1, turned_first, (2, 1, 2))

    @pl.when(south)
    def _():
        sums[rows - 1 :] = conv_rows(taps, rows - 1, 1, turned_first, (0, 1, 0))

    back_fields[...] = (cotangent[...].astype(jnp.float32) + sums[...]).astype(jnp.bfloat16)


def call(kernel, out_shapes, scratch, flops, *operands):
    vmem = pl.BlockSpec(memory_space=pltpu.VMEM)
    moved = sum(math.prod(v.shape) * v.dtype.itemsize for v in (*operands, *out_shapes))
    return pl.pallas_call(
        kernel,
        out_shape=out_shapes,
        in_specs=[pl.BlockSpec(memory_space=pltpu.SMEM)] + [vmem] * (len(operands) - 1),
        out_specs=[vmem] * len(out_shapes),
        scratch_shapes=[pltpu.VMEM(shape, dtype) for shape, dtype in scratch],
        compiler_params=pltpu.CompilerParams(vmem_limit_bytes=24 * 2**20),
        cost_estimate=pl.CostEstimate(flops=flops, bytes_accessed=moved, transcendentals=0),
    )(*operands)


def turned(weight):
    return jnp.transpose(weight[::-1, ::-1], (0, 1, 3, 2))


def by_row(weight):
    return weight.reshape(weight.shape[0], -1, weight.shape[-1])


def all_sum(kept, given, output, finish, operands):
    def exchange(v, axes):
        return lax.all_to_all(v, axes, 0, 0, tiled=True)

    def to_all(v, axes):
        return exchange(jnp.broadcast_to(v[None], (lax.axis_size(axes),) + v.shape), axes)

    def total(v):
        return jnp.sum(v.astype(jnp.float32), axis=0).astype(jnp.bfloat16)

    def other_core(v):
        return lax.ppermute(v, "core", [(0, 1), (1, 0)])

    channels = kept.shape[-1]
    kept, output = lax.optimization_barrier((kept + other_core(given), output))
    piece = kept.astype(jnp.bfloat16)
    piece = piece.reshape(lax.axis_size(SCATTER), -1, 4, channels)
    piece = total(exchange(piece, SCATTER))
    piece = total(to_all(piece, EXCHANGE))
    half = to_all(piece, SCATTER).reshape(-1, channels)
    half, operands = lax.optimization_barrier((half, operands))
    return half, other_core(half), output, finish(*operands)


def per_device(fields, cotangent, weight_first, weight_second):
    rows, cols, channels = fields.shape
    lat_place = lax.axis_index(LAT)
    north_pole = lat_place == 0
    south_pole = lat_place == lax.axis_size(LAT) - 1
    low_core = lax.axis_index("core") == 0
    flags = jnp.stack([north_pole, south_pole, low_core, low_core]).astype(jnp.int32)
    edges = halo_of_two(jnp.stack([fields, cotangent]), north_pole, south_pole)
    turned_first = by_row(turned(weight_first))
    edges, turned_first = lax.optimization_barrier((edges, turned_first))
    wide = -(-(cols + 2) // 8) * 8
    taps = 3 * channels
    flops = 2 * rows * cols * channels * channels * 9
    half = jax.ShapeDtypeStruct((9 * channels, channels), jnp.float32)
    bf16, f32 = jnp.bfloat16, jnp.float32
    ring, hidden_taps, kept, given = call(
        ring_kernel,
        (
            jax.ShapeDtypeStruct((rows + 2, wide, channels), bf16),
            jax.ShapeDtypeStruct((rows + 2, cols, taps), bf16),
            half,
            half,
        ),
        (
            ((2, rows + 4, wide + 8, channels), f32),
            ((2, rows + 4, wide, taps), bf16),
            ((2, rows + 2, wide, channels), f32),
            ((2, rows + 2, wide, channels), f32),
            ((rows + 2, cols, taps), bf16),
        ),
        4 * flops,
        flags, fields, cotangent, *edges, by_row(weight_first), by_row(turned(weight_second)),
    )
    block = jax.ShapeDtypeStruct(fields.shape, bf16)

    (output,) = call(
        output_kernel, (block,), (), flops, flags, hidden_taps, fields, by_row(weight_second)
    )

    def finish(*operands):
        return call(
            back_kernel,
            (block,),
            (
                ((rows + 2, wide, channels), f32),
                ((rows + 2, cols, taps), bf16),
                ((rows, cols, channels), f32),
            ),
            flops,
            *operands,
        )

    mine, theirs, output, (back_fields,) = all_sum(
        kept, given, output, finish, (flags, ring, cotangent, turned_first)
    )
    cells_total = rows * lax.axis_size(LAT) * cols * lax.axis_size(LON)
    grad_scale = 1.0 / math.sqrt(cells_total)
    grad_first, grad_second = (
        (jnp.where(low_core, one, other).astype(f32) * grad_scale).reshape(weight_first.shape)
        for one, other in ((mine, theirs), (theirs, mine))
    )
    return (output, back_fields, grad_first, grad_second)


def solution(mesh):
    fine = Mesh(mesh.devices.reshape(tuple(SIZES.values())), tuple(SIZES))
    cells = P(LAT, LON, None)
    return jax.shard_map(
        per_device,
        mesh=fine,
        in_specs=(cells, cells, P(), P()),
        out_specs=(cells, cells, P(), P()),
        check_vma=False,
    )
```
